128 devices in a mesh: row: 8 (over z_lo, y), col: 16 (over z_hi, x, core).
Axes of the slice: x: 4, y: 4, z: 4 (z_hi: 2, z_lo: 2; z = z_hi * 2 + z_lo), core: 2. Of those that a mesh axis runs over, the one named last changes fastest.
Arguments:
- density: float32 [6144, 6144], P('row', 'col'), may hold values from -1 to 1, as said below
- response: float32 [6144, 6144], P('row', 'col'), may hold values from -1 to 1, as said below
- density_mask: int32 [48, 48], replicated, may hold values from 0 to 1, as said below
- response_mask: int32 [48, 48], replicated, may hold values from 0 to 1, as said below
- branch: int32 [48], replicated, may hold values from 0 to 1
Outputs:
- new_density: float32 [6144, 6144], P('row', 'col')
- new_response: float32 [6144, 6144], P('row', 'col')
The draws below stay inside these ranges and needn't reach their ends.
Inputs may be any that keep to these rules, and one draw needn't show every extreme that they name: `density`: symmetric: equal to its own transpose. `response`: symmetric: equal to its own transpose. `density_mask`: symmetric, with ones on the diagonal. `response_mask`: symmetric, with ones on the diagonal.
All inputs are finite; a program needn't handle non-finite values.
Results may differ from the reference program's by a relative error of at most 0.000067.
Values sent between devices are 32-bit elements; how exact they have to be, the bound alone decides.
No kernel may reach another device: no remote copies, remote signals or barrier semaphores. Data moves between devices by JAX's collectives and lax.ppermute only.
A program may use at most 192 MiB of HBM per device.

```python
import math
import jax
import jax.numpy as jnp
from jax import lax

N = 6144
BLOCK = 128
NB = 48


def pattern(key):
    coins = jax.random.randint(key, (NB, NB), 0, 2, jnp.int32)
    row_ids = lax.broadcasted_iota(jnp.int32, (NB, NB), 0)
    col_ids = lax.broadcasted_iota(jnp.int32, (NB, NB), 1)
    coins = jnp.where(row_ids <= col_ids, coins, coins.T)
    return jnp.where(row_ids == col_ids, 1, coins).astype(jnp.int32)


def draw_density_mask(key, part):
    return pattern(jax.random.fold_in(key, 11))


def draw_response_mask(key, part):
    return pattern(jax.random.fold_in(key, 12))


def draw_density(key, part):
    first_key = jax.random.fold_in(jax.random.fold_in(key, 21), 0)
    gauss = jax.random.normal(first_key, (N, N), jnp.float32)
    factor = (N / 2.0) ** (-0.25)
    return jnp.clip((gauss + gauss.T) * (factor * math.sqrt(0.5)), -1.0, 1.0)


def draw_response(key, part):
    first_key = jax.random.fold_in(jax.random.fold_in(key, 22), 0)
    gauss = jax.random.normal(first_key, (N, N), jnp.float32)
    factor = (N / 2.0) ** (-0.25)
    return jnp.clip((gauss + gauss.T) * (factor * math.sqrt(0.5)), -1.0, 1.0)


def touch_ends(drawn, key, smallest, top_value):
    place = [jax.random.randint(jax.random.fold_in(key, axis), (), 0, length) for axis, length in enumerate(drawn.shape)]
    main_axis = drawn.shape.index(max(drawn.shape))
    beside = place[:main_axis] + [(place[main_axis] + 1) % drawn.shape[main_axis]] + place[main_axis + 1:]
    return drawn.at[tuple(place)].set(smallest).at[tuple(beside)].set(top_value)


def setup_inputs(seed: int = 0) -> dict:
    splits = jax.random.split(jax.random.key(seed), 6)
    return {
        "density": draw_density(jax.random.fold_in(splits[5], 71), 0),
        "response": draw_response(jax.random.fold_in(splits[5], 71), 0),
        "density_mask": draw_density_mask(jax.random.fold_in(splits[5], 71), 0),
        "response_mask": draw_response_mask(jax.random.fold_in(splits[5], 71), 0),
        "branch": touch_ends(jax.random.randint(splits[4], (NB,), 0, 2), jax.random.fold_in(splits[4], 1), 0, 1).astype(jnp.int32),
    }


def expand_mask(block_mask):
    return jnp.repeat(jnp.repeat(block_mask, BLOCK, 0), BLOCK, 1).astype(jnp.float32)


def reference(density, response, density_mask, response_mask, branch):
    masked_density = density * expand_mask(density_mask)
    masked_response = response * expand_mask(response_mask)
    square = jnp.dot(masked_density, masked_density, precision=lax.Precision.HIGHEST, preferred_element_type=jnp.float32)
    product = jnp.dot(masked_density, masked_response, precision=lax.Precision.HIGHEST, preferred_element_type=jnp.float32)
    combined = product + product.T
    chosen = jnp.repeat(branch, BLOCK)[:, None]
    new_density = jnp.where(chosen == 0, square, 2.0 * masked_density - square)
    new_response = jnp.where(chosen == 0, combined, 2.0 * masked_response - combined)
    return new_density, new_response
```

```python
import jax
import jax.numpy as jnp
from jax import lax
from jax.experimental import pallas as pl
from jax.experimental.pallas import tpu as pltpu
from jax.sharding import PartitionSpec as P

BLOCK = 128
AXES = ("row", "col")
F32 = jnp.float32


def device(x, y, z, c):
    return ((z % 2) * 4 + y) * 16 + (z // 2) * 8 + x * 2 + c


def moves(rule):
    pairs = []
    for x in range(4):
        for y in range(4):
            for z in range(4):
                for c in range(2):
                    to = rule(x, y, z, c)
                    if to is not None:
                        pairs.append((device(x, y, z, c), device(*to)))
    return pairs


X_UP = moves(lambda x, y, z, c: ((x + 1) % 4, y, z, c))
X_DN = moves(lambda x, y, z, c: ((x - 1) % 4, y, z, c))
Y_UP = moves(lambda x, y, z, c: (x, (y + 1) % 4, z, c))
Y_DN = moves(lambda x, y, z, c: (x, (y - 1) % 4, z, c))
CORE = moves(lambda x, y, z, c: (x, y, z, 1 - c))
PAIR = moves(lambda x, y, z, c: (x, y, z ^ 1, c))
Z_OUT = moves(lambda x, y, z, c: {1: (x, y, 0, c), 2: (x, y, 3, c)}.get(z))
Z_MID = moves(lambda x, y, z, c: {1: (x, y, 2, c), 2: (x, y, 1, c)}.get(z))
Z_WRAP = moves(lambda x, y, z, c: {0: (x, y, 3, c), 3: (x, y, 0, c)}.get(z))
Z_IN = moves(lambda x, y, z, c: {0: (x, y, 1, c), 3: (x, y, 2, c)}.get(z))
FLIP_Z = {0: 0, 1: 2, 2: 1, 3: 3}
SWAP = moves(lambda x, y, z, c: (y, x, FLIP_Z[z], c))
SWAP_CORE = moves(lambda x, y, z, c: (y, x, FLIP_Z[z], 1 - c))


def send(value, pairs):
    return lax.ppermute(value, AXES, pairs)


def after(value, *deps):
    return lax.optimization_barrier((value,) + deps)[0]


def vmem_spec():
    return pl.BlockSpec(memory_space=pltpu.VMEM)


def smem_spec():
    return pl.BlockSpec(memory_space=pltpu.SMEM)


def masked_block(ref, mask_ref, pos_ref, i, j):
    factor = mask_ref[pos_ref[0] + i, pos_ref[1] + j].astype(F32)
    return ref[i * BLOCK:(i + 1) * BLOCK, j * BLOCK:(j + 1) * BLOCK] * factor


def prepare_kernel(pos, dmask, rmask, dens, resp, ta, tb, dkeep, dsend, rkeep, rsend, scr):
    core = pos[2]
    mine = pl.multiple_of(core * 384, 384)
    other = pl.multiple_of((1 - core) * 384, 384)
    for src, mask, keep, away in ((resp, rmask, rkeep, rsend), (dens, dmask, dkeep, dsend)):
        for i in range(6):
            for j in range(3):
                scr[i * BLOCK:(i + 1) * BLOCK, j * BLOCK:(j + 1) * BLOCK] = masked_block(src, mask, pos, i, j)
        keep[...] = scr[pl.ds(mine, 384), :]
        away[...] = scr[pl.ds(other, 384), :]
    ta[0:192, :] = scr[0:192, :]
    ta[192:384, :] = scr[384:576, :]
    tb[0:192, :] = scr[192:384, :]
    tb[192:384, :] = scr[576:768, :]


def prepare(pos, dmask, rmask, dens, resp):
    half = jax.ShapeDtypeStruct((384, 384), F32)
    return pl.pallas_call(
        prepare_kernel,
        out_shape=[half] * 6,
        in_specs=[smem_spec()] * 3 + [vmem_spec()] * 2,
        out_specs=[vmem_spec()] * 6,
        scratch_shapes=[pltpu.VMEM((768, 384), F32)],
        name="prepare",
    )(pos, dmask, rmask, dens, resp)


def product_kernel(pos, a0, a1, a2, a2b, a3, b0, b1, b2, b2b, b3, keep, away, af, bf, ah, al, bh, bl, sem):
    copies_a = (
        ((a0, af.at[:, 0:384]),),
        ((a1, af.at[:, 384:768]),),
        ((a2, af.at[0:192, 768:1152]), (a2b, af.at[192:384, 768:1152])),
        ((a3, af.at[:, 1152:1536]),),
    )
    copies_b = (
        ((b0, bf.at[0]),),
        ((b1, bf.at[1]),),
        ((b2, bf.at[2, 0:192]), (b2b, bf.at[2, 192:384])),
        ((b3, bf.at[3]),),
    )
    n = 0
    waits = []
    for group in copies_b + copies_a:
        descs = []
        for src, dst in group:
            desc = pltpu.make_async_copy(src, dst, sem.at[n])
            desc.start()
            descs.append(desc)
            n += 1
        waits.append(descs)
    shift = pos[3]
    for descs in waits[:4]:
        for desc in descs:
            desc.wait()
    for k in range(4):
        value = bf[(shift + k) % 4]
        high = value.astype(jnp.bfloat16)
        bh[k * 384:(k + 1) * 384, :] = high
        bl[k * 384:(k + 1) * 384, :] = (value - high.astype(F32)).astype(jnp.bfloat16)
    for k in range(4):
        for desc in waits[4 + k]:
            desc.wait()
        value = af[:, k * 384:(k + 1) * 384]
        high = value.astype(jnp.bfloat16)
        ah[:, k * 384:(k + 1) * 384] = high
        al[:, k * 384:(k + 1) * 384] = (value - high.astype(F32)).astype(jnp.bfloat16)

    def dot(left, right):
        return jnp.dot(left, right, preferred_element_type=F32)

    for out, lo in ((away, 384), (keep, 0)):
        cols = slice(lo, lo + 384)
        high = bh[:, cols]
        out[...] = dot(al[...], high) + dot(ah[...], bl[:, cols]) + dot(ah[...], high)


def product(pos, a, b):
    any_spec = pl.BlockSpec(memory_space=pl.ANY)
    half = jax.ShapeDtypeStruct((384, 384), F32)
    return pl.pallas_call(
        product_kernel,
        out_shape=[half] * 2,
        in_specs=[smem_spec()] + [any_spec] * 10,
        out_specs=[vmem_spec()] * 2,
        scratch_shapes=[
            pltpu.VMEM((384, 1536), F32),
            pltpu.VMEM((4, 384, 768), F32),
            pltpu.VMEM((384, 1536), jnp.bfloat16),
            pltpu.VMEM((384, 1536), jnp.bfloat16),
            pltpu.VMEM((1536, 768), jnp.bfloat16),
            pltpu.VMEM((1536, 768), jnp.bfloat16),
            pltpu.SemaphoreType.DMA((10,)),
        ],
        cost_estimate=pl.CostEstimate(flops=2 * 3 * 384 * 1536 * 768, transcendentals=0, bytes_accessed=8_000_000),
        name="product",
    )(pos, *a, *b)


def combine_kernel(pos, keep, crecv, zrecv, total, same, flip):
    total[...] = keep[...] + crecv[...] + zrecv[...]
    core = pos[2]
    same[...] = total[pl.ds(pl.multiple_of(core * 192, 192), 192), :]
    flip[...] = total[pl.ds(pl.multiple_of((1 - core) * 192, 192), 192), :]


def combine(pos, keep, crecv, zrecv):
    return pl.pallas_call(
        combine_kernel,
        out_shape=[jax.ShapeDtypeStruct((r, 384), F32) for r in (384, 192, 192)],
        in_specs=[smem_spec()] + [vmem_spec()] * 3,
        out_specs=[vmem_spec()] * 3,
        name="combine",
    )(pos, keep, crecv, zrecv)


def finish_block(pos, branch, mask, raw, out, i, value):
    rows = slice(i * BLOCK, (i + 1) * BLOCK)
    chosen = branch[pos[0] + i] == 0
    for j in range(3):
        cols = slice(j * BLOCK, (j + 1) * BLOCK)
        part = value[:, cols]
        out[rows, cols] = jnp.where(chosen, part, 2.0 * masked_block(raw, mask, pos, i, j) - part)


def density_kernel(pos, branch, mask, raw, k1, c1, z1, k2, c2, z2, out, scr):
    for chunk, parts in enumerate(((k1, c1, z1), (k2, c2, z2))):
        for h in range(2):
            rows = slice(h * 192, (h + 1) * 192)
            at = h * 384 + chunk * 192
            scr[at:at + 192, :] = parts[0][rows, :] + parts[1][rows, :] + parts[2][rows, :]
    for i in range(6):
        finish_block(pos, branch, mask, raw, out, i, scr[i * BLOCK:(i + 1) * BLOCK, :])


def finish_density(pos, branch, mask, raw, *parts):
    return pl.pallas_call(
        density_kernel,
        out_shape=jax.ShapeDtypeStruct((768, 384), F32),
        in_specs=[smem_spec()] * 3 + [vmem_spec()] * 7,
        out_specs=vmem_spec(),
        scratch_shapes=[pltpu.VMEM((768, 384), F32)],
        name="finish_density",
    )(pos, branch, mask, raw, *parts)


def response_kernel(pos, branch, mask, raw, p1, p2, s1, s2, f1, f2, out, scr, xs):
    core = pos[2]
    xs[core, 0:192, :] = s1[...]
    xs[core, 192:384, :] = s2[...]
    xs[1 - core, 0:192, :] = f1[...]
    xs[1 - core, 192:384, :] = f2[...]
    for h in range(2):
        turned = xs[h].T
        rows = slice(h * 192, (h + 1) * 192)
        scr[h * 384:h * 384 + 192, :] = p1[rows, :] + turned[0:192, :]
        scr[h * 384 + 192:h * 384 + 384, :] = p2[rows, :] + turned[192:384, :]
    for i in range(6):
        finish_block(pos, branch, mask, raw, out, i, scr[i * BLOCK:(i + 1) * BLOCK, :])


def finish_response(pos, branch, mask, raw, *parts):
    return pl.pallas_call(
        response_kernel,
        out_shape=jax.ShapeDtypeStruct((768, 384), F32),
        in_specs=[smem_spec()] * 3 + [vmem_spec()] * 7,
        out_specs=vmem_spec(),
        scratch_shapes=[pltpu.VMEM((768, 384), F32), pltpu.VMEM((2, 384, 384), F32)],
        name="finish_response",
    )(pos, branch, mask, raw, *parts)


def ring(tile, up_pairs, dn_pairs):
    half = tile.shape[0] // 2
    up = send(tile, up_pairs)
    dn = send(tile, dn_pairs)
    far1 = send(up[:half], up_pairs)
    far2 = send(dn[half:], dn_pairs)
    return tile, dn, far1, far2, up


def per_device(density, response, density_mask, response_mask, branch):
    row = lax.axis_index("row")
    col = lax.axis_index("col")
    y, x, core = row % 4, (col // 2) % 4, col % 2
    z = (col // 8) * 2 + row // 4
    pos = jnp.stack([row * 6, col * 3, core, (x - y) % 4]).astype(jnp.int32)
    ta, tb, dkeep, dsend, rkeep, rsend = prepare(pos, density_mask, response_mask, density, response)

    outer = (z == 0) | (z == 3)

    def first(t):
        return send(t, Z_OUT) + send(t, Z_MID)

    def second(t):
        return jnp.where(outer, t, send(send(t, Z_WRAP), Z_IN))

    r_own = jnp.concatenate([rkeep, send(rsend, CORE)], axis=1)
    d_own = jnp.concatenate([dkeep, send(dsend, CORE)], axis=1)
    b_r = ring(r_own, Y_UP, Y_DN)
    b_d = ring(after(d_own, b_r[1], b_r[4]), Y_UP, Y_DN)

    s1a = first(ta)
    s2a = second(ta)
    tb1 = after(tb, s1a, s2a)
    s1b = first(tb1)
    s2b = second(tb1)
    a1 = ring(s1a, X_UP, X_DN)
    a2 = ring(after(s2a, a1[1], a1[4]), X_UP, X_DN)
    a3 = ring(after(s1b, a2[1], a2[4]), X_UP, X_DN)
    a4 = ring(after(s2b, a3[1], a3[4]), X_UP, X_DN)

    def partner(a, b):
        keep, away = product(pos, a, b)
        return send(keep + send(away, CORE), PAIR)

    def own(a, b):
        keep, away = product(pos, a, b)
        return keep, send(away, CORE)

    def swap(parts):
        total, same, flip = combine(pos, *parts)
        return total, send(same, SWAP), send(flip, SWAP_CORE)

    zp_a = partner(a1, b_r)
    p_a, same_a, flip_a = swap(own(a2, b_r) + (zp_a,))
    zp_b = partner(a3, b_r)
    zs_a = partner(a1, b_d)
    p_b, same_b, flip_b = swap(own(a4, b_r) + (zp_b,))
    zs_b = partner(a3, b_d)
    s_a = own(a2, b_d) + (zs_a,)
    s_b = own(a4, b_d) + (zs_b,)
    new_density = finish_density(pos, branch, density_mask, density, *s_a, *s_b)
    new_response = finish_response(
        pos, branch, response_mask, response, p_a, p_b, same_a, same_b, flip_a, flip_b
    )
    return new_density, new_response


def solution(mesh):
    return jax.shard_map(
        per_device,
        mesh=mesh,
        in_specs=(P("row", "col"), P("row", "col"), P(), P(), P()),
        out_specs=(P("row", "col"), P("row", "col")),
        check_vma=False,
    )
```
